512 devices in a mesh: col: 64 (over y, x, z_lo), row: 8 (over z_hi, core).
Axes of the slice: x: 4, y: 4, z: 16 (z_hi: 4, z_lo: 4; z = z_hi * 4 + z_lo), core: 2. Of those that a mesh axis runs over, the one named last changes fastest.
Arguments:
- slab_embed: float32 [64, 4096], P(None, 'row'), may hold values from -6 to 6
- slab_probe: float32 [32, 4096], P(None, 'row'), may hold values from -6 to 6
- point_embed: float32 [64, 131072], P(None, 'col'), may hold values from -6 to 6
- point_probe: float32 [32, 131072], P(None, 'col'), may hold values from -1.2 to 1.2
- inv_scale: float32 [64], replicated, may hold values from 0.08 to 0.3
Outputs:
- slab_grad: float32 [64, 4096], P(None, 'row')
- point_grad: float32 [64, 131072], P(None, 'col')
The draws below stay inside these ranges and needn't reach their ends.
All inputs are finite; a program needn't handle non-finite values.
Results may differ from the reference program's by a relative error of at most 0.0001.
Values sent between devices are 32-bit elements; how exact they have to be, the bound alone decides.
A program may use at most 64 MiB of HBM per device.

```python
import math
import jax
import jax.numpy as jnp
from jax import lax

EMB = 64
PROBES = 32
SLAB = 4096
NPTS = 131072


def levels(rng, extent, cuts, low, high):
    def one(axis_at, parts):
        heights = jax.random.uniform(jax.random.fold_in(jax.random.fold_in(rng, 6), axis_at), (parts,), jnp.float32, low / len(cuts), high / len(cuts))
        return jnp.repeat(jnp.exp(heights), extent[axis_at] // parts).reshape((-1,) + (1,) * (len(extent) - axis_at - 1))

    level = one(*cuts[0])
    for cut in cuts[1:]:
        level = level * one(*cut)
    return level


def centred(own_key, extent, deviation, limit, shards=(), held_as=jnp.bfloat16):
    drawn = deviation * jax.random.normal(own_key, extent, jnp.float32)
    if shards:
        drawn = drawn * levels(own_key, extent, shards, -0.22, 0.18)
    return jnp.clip(drawn, -limit, limit).astype(held_as)


def setup_inputs(seed: int = 0) -> dict:
    splits = jax.random.split(jax.random.key(seed), 6)
    slab_embed = centred(splits[0], (EMB, SLAB), 1.0, 6.0, ((1, 8),), jnp.float32)
    slab_probe = centred(splits[1], (PROBES, SLAB), 1.0, 6.0, ((1, 8),), jnp.float32)
    point_embed = centred(splits[2], (EMB, NPTS), 1.0, 6.0, ((1, 64),), jnp.float32)
    point_probe = centred(splits[3], (PROBES, NPTS), 0.2, 1.2, ((1, 64),), jnp.float32)
    inv_scale = jnp.clip(jnp.exp(jax.random.uniform(splits[4], (EMB,), jnp.float32, math.log(0.08), math.log(0.3))), 0.08, 0.3)
    return dict(slab_embed=slab_embed, slab_probe=slab_probe, point_embed=point_embed, point_probe=point_probe, inv_scale=inv_scale)


def reference(slab_embed, slab_probe, point_embed, point_probe, inv_scale):
    hp = lax.Precision.HIGHEST
    weight_sq = inv_scale * inv_scale
    scaled = slab_embed * weight_sq[:, None]
    self_term = jnp.sum(scaled * slab_embed, axis=0)
    width = min(4096, NPTS)
    count = NPTS // width
    embed_blocks = point_embed.reshape(EMB, count, width).transpose(1, 0, 2)
    probe_blocks = point_probe.reshape(PROBES, count, width).transpose(1, 0, 2)

    def step(carry, item):
        row_total, mixed = carry
        points, probes = item
        other_term = jnp.sum(weight_sq[:, None] * points * points, axis=0)
        cross = jnp.dot(scaled.T, points, precision=hp)
        kernel = jnp.exp(-0.5 * (self_term[:, None] + other_term[None, :] - 2.0 * cross))
        weights = kernel * jnp.dot(slab_probe.T, probes, precision=hp)
        row_total = row_total + jnp.sum(weights, axis=1)
        mixed = mixed + jnp.dot(points, weights.T, precision=hp)
        grad_block = weight_sq[:, None] * (jnp.dot(slab_embed, weights, precision=hp) - points * jnp.sum(weights, axis=0)[None, :])
        return (row_total, mixed), grad_block

    start = (jnp.zeros((SLAB,), jnp.float32), jnp.zeros((EMB, SLAB), jnp.float32))
    (row_total, mixed), grads = lax.scan(step, start, (embed_blocks, probe_blocks))
    slab_grad = -weight_sq[:, None] * (slab_embed * row_total[None, :] - mixed)
    point_grad = grads.transpose(1, 0, 2).reshape(EMB, NPTS)
    return slab_grad, point_grad
```

```python
import math

import jax
import jax.numpy as jnp
from jax import lax
from jax.experimental import pallas as pl
from jax.experimental.pallas import tpu as pltpu
from jax.sharding import PartitionSpec as P

MESH = pl.DeviceIdType.MESH
F32 = jnp.float32
BF16 = jnp.bfloat16
LOG2E = math.log2(math.e)
EMB = 64
PROBES = 32
ROWS = 512
PIECE = 512
UNIT = 256
HALF = 32


def split3(v):
    high = v.astype(BF16)
    rest = v - high.astype(F32)
    mid = rest.astype(BF16)
    low = (rest - mid.astype(F32)).astype(BF16)
    return high, mid, low


def matmul(a, b, contract):
    return lax.dot_general(a, b, ((contract[:1], contract[1:]), ((), ())), preferred_element_type=F32)


def kernel(
    scale_ref,
    slab_ref,
    slab_probe_ref,
    point_ref,
    point_probe_ref,
    slab_out,
    point_out,
    left_c,
    left_p,
    left_s,
    part,
    sib_in,
    r1,
    r2,
    full,
    sp,
    sx_in,
    sx,
    sy_in,
    sz,
    sf,
    send,
    recv,
):
    row, col = lax.axis_index("row"), lax.axis_index("col")
    core, q = lax.rem(row, 2), row // 2
    zl, x, y = lax.rem(col, 4), lax.rem(col // 4, 4), col // 16
    other = 1 - core

    def at_z(k):
        return (col, lax.rem(q + k, 4) * 2 + core)

    sibling = (col, q * 2 + other)
    z_up, z_down = at_z(1), at_z(3)

    def at_x(k):
        return (y * 16 + lax.rem(x + k, 4) * 4 + zl, row)

    def at_y(k):
        return (lax.rem(y + k, 4) * 16 + x * 4 + zl, row)

    def at_l(k):
        return (y * 16 + x * 4 + lax.rem(zl + k, 4), row)

    partners = [sibling, z_up, z_down]
    for k in (1, 2, 3):
        partners += [at_x(k), at_y(k), at_l(k)]
    barrier = pltpu.get_barrier_semaphore()
    for device in partners:
        pl.semaphore_signal(barrier, inc=1, device_id=device, device_id_type=MESH)

    count = [0]

    def copy(src, dst, device):
        i = count[0]
        count[0] += 1
        return pltpu.make_async_remote_copy(
            src_ref=src, dst_ref=dst, send_sem=send.at[i], recv_sem=recv.at[i],
            device_id=device, device_id_type=MESH,
        )

    diag = lax.broadcasted_iota(jnp.int32, (EMB, EMB), 0) == lax.broadcasted_iota(jnp.int32, (EMB, EMB), 1)
    scale = jnp.sum(jnp.where(diag, scale_ref[...], 0.0), axis=1, keepdims=True)
    w2 = scale * scale
    slab = slab_ref[...]
    scaled = slab * w2
    self_term = jnp.sum(scaled * slab, axis=0, keepdims=True) * (-0.5 * LOG2E)
    xh, xm, xl = split3(scaled * LOG2E)
    lane_id = lax.broadcasted_iota(jnp.int32, (16, ROWS), 0)

    def extras(term, first):
        th, tm, tl = (t.astype(F32) for t in split3(term))
        base = jnp.where(lane_id < 6, 1.0, 0.0)
        base = jnp.where(lane_id == first, th, base)
        base = jnp.where(lane_id == first + 1, tm, base)
        base = jnp.where(lane_id == first + 2, tl, base)
        return base.astype(BF16)

    left_c[...] = jnp.concatenate([xh, xh, xm, xh, xl, xm, extras(self_term, 0)], axis=0).T
    ph, pm, pl_ = split3(slab_probe_ref[...])
    left_p[...] = jnp.concatenate([ph, ph, pm, ph, pl_, pm], axis=0).T
    sh, sm, sl = split3(slab)
    ones = jnp.ones((16, ROWS), BF16)
    left_s[...] = jnp.concatenate([sh, sm, sl, ones], axis=0)

    def compute(j, piece, total):
        for u in range(2):
            cols = pl.ds(pl.multiple_of(piece * PIECE + u * UNIT, UNIT), UNIT)
            points = point_ref[:, cols]
            probes = point_probe_ref[:, cols]
            other_term = jnp.sum(w2 * points * points, axis=0, keepdims=True) * (-0.5 * LOG2E)
            yh, ym, yl = split3(points)
            th, tm, tl = (t.astype(F32) for t in split3(other_term))
            ids = lane_id[:, :UNIT]
            base = jnp.where(ids < 6, 1.0, 0.0)
            base = jnp.where(ids == 3, th, base)
            base = jnp.where(ids == 4, tm, base)
            base = jnp.where(ids == 5, tl, base)
            right_c = jnp.concatenate([yh, ym, yh, yl, yh, ym, base.astype(BF16)], axis=0)
            gh, gm, gl = split3(probes)
            right_p = jnp.concatenate([gh, gm, gh, gl, gh, gm], axis=0)
            exponent = matmul(left_c[...], right_c, (1, 0))
            weights = jnp.exp2(exponent) * matmul(left_p[...], right_p, (1, 0))
            mh = weights.astype(BF16)
            ml = (weights - mh.astype(F32)).astype(BF16)
            ls = left_s[...]
            o2 = matmul(ls, mh, (1, 0)) + matmul(ls, ml, (1, 0))
            right_s = jnp.concatenate([yh, ym, yl, ones[:, :UNIT]], axis=0)
            o1 = matmul(right_s, mh, (1, 1)) + matmul(right_s, ml, (1, 1))
            total = o1 if total is None else total + o1
            mixed = o2[0:64] + o2[64:128] + o2[128:192]
            terms = w2 * (mixed - points * o2[192:193])
            part[j, 0, u] = terms[:HALF]
            part[j, 1, u] = terms[HALF:]
        return total

    def to_sibling(j):
        c = copy(part.at[j, other], sib_in.at[j], sibling)
        c.start()
        return c

    def take_sibling(j, c):
        c.wait_recv()
        part[j, core] = part[j, core] + sib_in[j]

    done = []

    def go(src, dst, device):
        c = copy(src, dst, device)
        c.start()
        done.append(c)
        return c

    p_up, p_down, p_far = lax.rem(q + 1, 4), lax.rem(q + 3, 4), lax.rem(q + 2, 4)

    total = compute(0, p_far, None)
    pl.semaphore_wait(barrier, len(partners))
    s0 = to_sibling(0)
    total = compute(1, p_up, total)
    take_sibling(0, s0)
    a0 = go(part.at[0, core, 0], r1.at[0], z_down)
    a1 = go(part.at[0, core, 1], r1.at[1], z_up)
    s1 = to_sibling(1)
    total = compute(2, p_down, total)
    take_sibling(1, s1)
    b1 = go(part.at[1, core, 0], r2.at[1, 0], z_up)
    s2 = to_sibling(2)
    total = compute(3, q, total)
    take_sibling(2, s2)
    b0 = go(part.at[2, core, 1], r2.at[0, 1], z_down)
    s3 = to_sibling(3)

    slab_mixed = total[0:64] + total[64:128] + total[128:192]
    slab_terms = w2 * (slab_mixed - slab * total[192:193])
    for i in range(4):
        for k in range(4):
            sp[i, k] = slab_terms[16 * i : 16 * i + 16, 128 * k : 128 * k + 128]
    cx = [go(sp.at[lax.rem(x + k, 4)], sx_in.at[k - 1], at_x(k)) for k in (1, 2, 3)]

    take_sibling(3, s3)
    a0.wait_recv()
    part[2, core, 0] = part[2, core, 0] + r1[0]
    b2 = go(part.at[2, core, 0], r2.at[0, 0], z_down)
    a1.wait_recv()
    part[1, core, 1] = part[1, core, 1] + r1[1]
    b3 = go(part.at[1, core, 1], r2.at[1, 1], z_up)

    for c in cx:
        c.wait_recv()
    sx[...] = sp[x] + sx_in[0] + sx_in[1] + sx_in[2]
    cy = [go(sx.at[lax.rem(y + k, 4)], sy_in.at[k - 1], at_y(k)) for k in (1, 2, 3)]
    for c in cy:
        c.wait_recv()
    sz[zl] = sx[y] + sy_in[0] + sy_in[1] + sy_in[2]
    cl = [go(sz.at[zl], sz.at[zl], at_l(k)) for k in (1, 2, 3)]

    b0.wait_recv()
    b1.wait_recv()
    b2.wait_recv()
    full[q, core, 0] = part[3, core, 0] + r2[0, 0] + r2[1, 0]
    d0 = go(full.at[q, core, 0], full.at[q, core, 0], z_down)
    b3.wait_recv()
    full[q, core, 1] = part[3, core, 1] + r2[0, 1] + r2[1, 1]
    d1 = go(full.at[q, core, 1], full.at[q, core, 1], z_up)
    d2 = go(full.at[q, core, 0], full.at[q, core, 0], z_up)
    d3 = go(full.at[q, core, 1], full.at[q, core, 1], z_down)
    e = [go(full.at[q, core], full.at[q, core], sibling)]

    for c in cl:
        c.wait_recv()
    sf[x, y] = sz[0] + sz[1] + sz[2] + sz[3]
    cy = [go(sf.at[x, y], sf.at[x, y], at_y(k)) for k in (1, 2, 3)]

    d0.wait_recv()
    f0 = go(full.at[p_up, core, 0], full.at[p_up, core, 0], z_down)
    d1.wait_recv()
    f1 = go(full.at[p_down, core, 1], full.at[p_down, core, 1], z_up)
    for c in cy:
        c.wait_recv()
    cx = [go(sf.at[x], sf.at[x], at_x(k)) for k in (1, 2, 3)]
    d2.wait_recv()
    e.append(go(full.at[p_down, core], full.at[p_down, core], sibling))
    d3.wait_recv()
    e.append(go(full.at[p_up, core], full.at[p_up, core], sibling))
    f0.wait_recv()
    e.append(go(full.at[p_far, core, 0], full.at[p_far, core, 0], sibling))
    f1.wait_recv()
    e.append(go(full.at[p_far, core, 1], full.at[p_far, core, 1], sibling))

    for c in cx:
        c.wait_recv()
    for i in range(4):
        for k in range(4):
            slab_out[16 * i : 16 * i + 16, 128 * k : 128 * k + 128] = sf[i, k]
    for c in e:
        c.wait_recv()
    for o in range(4):
        for h in range(2):
            for u in range(2):
                lo = o * PIECE + u * UNIT
                point_out[h * HALF : h * HALF + HALF, lo : lo + UNIT] = full[o, h, u]
    for c in [s0, s1, s2, s3] + done:
        c.wait_send()


def local(slab_embed, slab_probe, point_embed, point_probe, inv_scale):
    vmem = pl.BlockSpec(memory_space=pltpu.VMEM)
    return pl.pallas_call(
        kernel,
        name="pathwise_grad",
        out_shape=(
            jax.ShapeDtypeStruct(slab_embed.shape, F32),
            jax.ShapeDtypeStruct(point_embed.shape, F32),
        ),
        in_specs=[vmem] * 5,
        out_specs=(vmem, vmem),
        scratch_shapes=[
            pltpu.VMEM((ROWS, 6 * EMB + 16), BF16),
            pltpu.VMEM((ROWS, 6 * PROBES), BF16),
            pltpu.VMEM((3 * EMB + 16, ROWS), BF16),
            pltpu.VMEM((4, 2, 2, HALF, UNIT), F32),
            pltpu.VMEM((4, 2, HALF, UNIT), F32),
            pltpu.VMEM((2, HALF, UNIT), F32),
            pltpu.VMEM((2, 2, HALF, UNIT), F32),
            pltpu.VMEM((4, 2, 2, HALF, UNIT), F32),
            pltpu.VMEM((4, 4, 16, 128), F32),
            pltpu.VMEM((3, 4, 16, 128), F32),
            pltpu.VMEM((4, 16, 128), F32),
            pltpu.VMEM((3, 16, 128), F32),
            pltpu.VMEM((4, 16, 128), F32),
            pltpu.VMEM((4, 4, 16, 128), F32),
            pltpu.SemaphoreType.DMA((40,)),
            pltpu.SemaphoreType.DMA((40,)),
        ],
        compiler_params=pltpu.CompilerParams(
            collective_id=0, has_side_effects=True, vmem_limit_bytes=40 * 1024 * 1024
        ),
    )(inv_scale.reshape(1, EMB), slab_embed, slab_probe, point_embed, point_probe)


def solution(mesh):
    placed = (P(None, "row"), P(None, "row"), P(None, "col"), P(None, "col"), P())
    return jax.shard_map(
        local,
        mesh=mesh,
        in_specs=placed,
        out_specs=(P(None, "row"), P(None, "col")),
        check_vma=False,
    )
```

```python
import math

import jax
import jax.numpy as jnp
from jax import lax
from jax.experimental import pallas as pl
from jax.experimental.pallas import tpu as pltpu
from jax.sharding import PartitionSpec as P

MESH = pl.DeviceIdType.MESH
F32 = jnp.float32
BF16 = jnp.bfloat16
LOG2E = math.log2(math.e)
EMB = 64
PROBES = 32
ROWS = 512
PIECE = 512
UNIT = 256
VMEM_MIB = 40
HALF = 32


def split3(v):
    high = v.astype(BF16)
    rest = v - high.astype(F32)
    mid = rest.astype(BF16)
    low = (rest - mid.astype(F32)).astype(BF16)
    return high, mid, low


def matmul(a, b, contract):
    return lax.dot_general(a, b, ((contract[:1], contract[1:]), ((), ())), preferred_element_type=F32)


def kernel(
    scale_hbm,
    slab_hbm,
    slab_probe_hbm,
    point_hbm,
    point_probe_hbm,
    slab_out,
    point_out,
    scale_ref,
    slab_ref,
    slab_probe_ref,
    point_ref,
    point_probe_ref,
    left_c,
    left_p,
    left_s,
    part,
    sib_in,
    r1,
    r2,
    full,
    sp,
    sx_in,
    sx,
    sy_in,
    sz,
    sf,
    load,
    send,
    recv,
):
    row, col = lax.axis_index("row"), lax.axis_index("col")
    core, q = lax.rem(row, 2), row // 2
    zl, x, y = lax.rem(col, 4), lax.rem(col // 4, 4), col // 16
    other = 1 - core
    p_up, p_down, p_far = lax.rem(q + 1, 4), lax.rem(q + 3, 4), lax.rem(q + 2, 4)
    pieces = (p_far, p_up, p_down, q)

    def columns(j, u):
        return pl.ds(pl.multiple_of(pieces[j] * PIECE + u * UNIT, UNIT), UNIT)

    loads = [
        pltpu.make_async_copy(scale_hbm, scale_ref, load.at[0]),
        pltpu.make_async_copy(slab_hbm, slab_ref, load.at[1]),
        pltpu.make_async_copy(slab_probe_hbm, slab_probe_ref, load.at[2]),
        pltpu.make_async_copy(point_hbm, point_ref, load.at[3]),
        pltpu.make_async_copy(point_probe_hbm, point_probe_ref, load.at[4]),
    ]
    for c in loads:
        c.start()

    def at_z(k):
        return (col, lax.rem(q + k, 4) * 2 + core)

    sibling = (col, q * 2 + other)
    z_up, z_down = at_z(1), at_z(3)

    def in_plane(i, k):
        return (lax.rem(y + k, 4) * 16 + lax.rem(x + i, 4) * 4 + zl, row)

    def at_l(k):
        return (y * 16 + x * 4 + lax.rem(zl + k, 4), row)

    partners = [sibling, z_up, z_down]
    for k in (1, 2, 3):
        partners += [in_plane(k, 0), in_plane(0, k), at_l(k)]
    barrier = pltpu.get_barrier_semaphore()
    for device in partners:
        pl.semaphore_signal(barrier, inc=1, device_id=device, device_id_type=MESH)

    sent = []

    def go(src, dst, device):
        i = len(sent)
        c = pltpu.make_async_remote_copy(
            src_ref=src, dst_ref=dst, send_sem=send.at[i], recv_sem=recv.at[i],
            device_id=device, device_id_type=MESH,
        )
        c.start()
        sent.append(c)
        return c

    diag = lax.broadcasted_iota(jnp.int32, (EMB, EMB), 0) == lax.broadcasted_iota(jnp.int32, (EMB, EMB), 1)
    row_id = lax.broadcasted_iota(jnp.int32, (16, ROWS), 0)
    ones = jnp.ones((16, ROWS), BF16)

    def extras(term, first, width):
        ids = row_id[:, :width]
        base = jnp.where(ids < 6, 1.0, 0.0)
        for i, t in enumerate(split3(term)):
            base = jnp.where(ids == first + i, t.astype(F32), base)
        return base.astype(BF16)

    loads[0].wait()
    loads[1].wait()
    scale = jnp.sum(jnp.where(diag, scale_ref[...], 0.0), axis=1, keepdims=True)
    w2 = scale * scale
    slab = slab_ref[...]
    scaled = slab * w2
    self_term = jnp.sum(scaled * slab, axis=0, keepdims=True) * (-0.5 * LOG2E)
    xh, xm, xl = split3(scaled * LOG2E)
    hm = jnp.concatenate([xh, xm], axis=0).T
    left_c[:, 0:128] = hm
    left_c[:, 128:256] = hm
    left_c[:, 256:384] = jnp.concatenate([xh, xl], axis=0).T
    left_c[:, 384:400] = extras(self_term, 0, ROWS).T
    loads[2].wait()
    ph, pm, pl_ = split3(slab_probe_ref[...])
    left_p[:, 0:128] = jnp.concatenate([ph, pm, ph, pm], axis=0).T
    left_p[:, 128:192] = jnp.concatenate([ph, pl_], axis=0).T
    sh, sm, sl = split3(slab)
    left_s[...] = jnp.concatenate([sh, sm, sl, ones], axis=0)
    loads[3].wait()
    loads[4].wait()

    def compute(u, j, total):
        points = point_ref[:, columns(j, u)]
        probes = point_probe_ref[:, columns(j, u)]
        other_term = jnp.sum(w2 * points * points, axis=0, keepdims=True) * (-0.5 * LOG2E)
        yh, ym, yl = split3(points)
        right_c = jnp.concatenate([yh, ym, ym, yh, yl, yh, extras(other_term, 3, UNIT)], axis=0)
        gh, gm, gl = split3(probes)
        right_p = jnp.concatenate([gh, gm, gm, gh, gl, gh], axis=0)
        exponent = matmul(left_c[...], right_c, (1, 0))
        weights = jnp.exp2(exponent) * matmul(left_p[...], right_p, (1, 0))
        mh = weights.astype(BF16)
        ml = (weights - mh.astype(F32)).astype(BF16)
        ls = left_s[...]
        o2 = matmul(jnp.concatenate([ls, ls], axis=1), jnp.concatenate([mh, ml], axis=0), (1, 0))
        right_s = jnp.concatenate([yh, ym, yl, ones[:, :UNIT]], axis=0)
        o1 = matmul(jnp.concatenate([right_s, right_s], axis=1), jnp.concatenate([mh, ml], axis=1), (1, 1))
        mixed = o2[0:64] + o2[64:128] + o2[128:192]
        terms = w2 * (mixed - points * o2[192:193])
        for h in range(2):
            for v in range(2):
                part[u, j, h, v] = terms[h * HALF : h * HALF + HALF, v * 128 : v * 128 + 128]
        return o1 if total is None else total + o1

    def to_sibling(u, j):
        return go(part.at[u, j, other], sib_in.at[u, j], sibling)

    def take(c, u, j):
        c.wait_recv()
        part[u, j, core] = part[u, j, core] + sib_in[u, j]

    def far(u):
        a0 = go(part.at[u, 0, core, 0], r1.at[u, 0], z_down)
        a1 = go(part.at[u, 0, core, 1], r1.at[u, 1], z_up)
        return a0, a1

    def near(u):
        b1 = go(part.at[u, 1, core, 0], r2.at[u, 1, 0], z_up)
        b0 = go(part.at[u, 2, core, 1], r2.at[u, 0, 1], z_down)
        return b0, b1

    def near_sum(u, a):
        a[0].wait_recv()
        part[u, 2, core, 0] = part[u, 2, core, 0] + r1[u, 0]
        b2 = go(part.at[u, 2, core, 0], r2.at[u, 0, 0], z_down)
        a[1].wait_recv()
        part[u, 1, core, 1] = part[u, 1, core, 1] + r1[u, 1]
        b3 = go(part.at[u, 1, core, 1], r2.at[u, 1, 1], z_up)
        return b2, b3

    def share(u, piece, device, v=None):
        block = full.at[u, piece, core] if v is None else full.at[u, piece, core, v]
        return go(block, block, device)

    def finish(u, b, c):
        b[1].wait_recv()
        c[0].wait_recv()
        full[u, q, core, 0] = part[u, 3, core, 0] + r2[u, 0, 0] + r2[u, 1, 0]
        d0 = share(u, q, z_down, 0)
        b[0].wait_recv()
        c[1].wait_recv()
        full[u, q, core, 1] = part[u, 3, core, 1] + r2[u, 0, 1] + r2[u, 1, 1]
        d1 = share(u, q, z_up, 1)
        return d0, d1

    def finish_rest(u, d):
        d2 = share(u, q, z_up, 0)
        d3 = share(u, q, z_down, 1)
        return d + (d2, d3), [share(u, q, sibling)]

    def forward(u, d):
        d[0].wait_recv()
        f0 = share(u, p_up, z_down, 0)
        d[1].wait_recv()
        f1 = share(u, p_down, z_up, 1)
        return f0, f1

    def spread(u, d, e):
        d[2].wait_recv()
        e.append(share(u, p_down, sibling))
        d[3].wait_recv()
        e.append(share(u, p_up, sibling))

    def spread_far(u, f, e):
        f[0].wait_recv()
        e.append(share(u, p_far, sibling, 0))
        f[1].wait_recv()
        e.append(share(u, p_far, sibling, 1))

    def store(u, piece):
        for h in range(2):
            for v in range(2):
                lo = pl.multiple_of(piece * PIECE + u * UNIT + v * 128, 128)
                point_out[h * HALF : h * HALF + HALF, pl.ds(lo, 128)] = full[u, piece, h, v]

    total = compute(0, 0, None)
    pl.semaphore_wait(barrier, len(partners))
    s00 = to_sibling(0, 0)
    total = compute(1, 0, total)
    s10 = to_sibling(1, 0)
    total = compute(0, 1, total)
    s01 = to_sibling(0, 1)
    take(s00, 0, 0)
    a_0 = far(0)
    total = compute(0, 2, total)
    s02 = to_sibling(0, 2)
    take(s10, 1, 0)
    a_1 = far(1)
    total = compute(1, 1, total)
    s11 = to_sibling(1, 1)
    take(s01, 0, 1)
    total = compute(1, 2, total)
    s12 = to_sibling(1, 2)
    take(s02, 0, 2)
    b_0 = near(0)
    total = compute(0, 3, total)
    s03 = to_sibling(0, 3)
    take(s11, 1, 1)
    total = compute(1, 3, total)
    s13 = to_sibling(1, 3)
    take(s12, 1, 2)
    b_1 = near(1)

    slab_mixed = total[0:64] + total[64:128] + total[128:192]
    slab_terms = w2 * (slab_mixed - slab * total[192:193])
    for i in range(4):
        for k in range(4):
            sp[i, k] = slab_terms[16 * i : 16 * i + 16, 128 * k : 128 * k + 128]
    across = [go(sp.at[lax.rem(x + k, 4)], sx_in.at[k - 1], in_plane(k, 0)) for k in (1, 2, 3)]
    c_0 = near_sum(0, a_0)
    c_1 = near_sum(1, a_1)
    take(s03, 0, 3)
    take(s13, 1, 3)
    for c in across:
        c.wait_recv()
    sx[...] = sp[x] + sx_in[0] + sx_in[1] + sx_in[2]
    across = [go(sx.at[lax.rem(y + k, 4)], sy_in.at[k - 1], in_plane(0, k)) for k in (1, 2, 3)]

    for c in across:
        c.wait_recv()
    sz[zl] = sx[y] + sy_in[0] + sy_in[1] + sy_in[2]
    along = [go(sz.at[zl], sz.at[zl], at_l(k)) for k in (1, 2, 3)]

    d_0 = finish(0, b_0, c_0)
    d_1 = finish(1, b_1, c_1)
    d_0, e_0 = finish_rest(0, d_0)
    d_1, e_1 = finish_rest(1, d_1)
    for c in along:
        c.wait_recv()
    sf[x, y] = sz[0] + sz[1] + sz[2] + sz[3]
    gather = [go(sf.at[x, y], sf.at[x, y], in_plane(0, k)) for k in (1, 2, 3)]
    f_0 = forward(0, d_0)
    f_1 = forward(1, d_1)
    for c in gather:
        c.wait_recv()
    gather = [go(sf.at[x], sf.at[x], in_plane(k, 0)) for k in (1, 2, 3)]
    spread(0, d_0, e_0)
    spread(1, d_1, e_1)
    for u, e in enumerate((e_0, e_1)):
        for c in e:
            c.wait_recv()
        for j in (1, 2, 3):
            store(u, pieces[j])
    spread_far(0, f_0, e_0)
    spread_far(1, f_1, e_1)
    for c in gather:
        c.wait_recv()
    for i in range(4):
        for k in range(4):
            slab_out[16 * i : 16 * i + 16, 128 * k : 128 * k + 128] = sf[i, k]
    for u, e in enumerate((e_0, e_1)):
        for c in e[3:]:
            c.wait_recv()
        store(u, p_far)
    for c in sent:
        c.wait_send()


def local(slab_embed, slab_probe, point_embed, point_probe, inv_scale):
    vmem = pl.BlockSpec(memory_space=pltpu.VMEM)
    hbm = pl.BlockSpec(memory_space=pltpu.HBM)
    shapes = (
        jax.ShapeDtypeStruct(slab_embed.shape, F32),
        jax.ShapeDtypeStruct(point_embed.shape, F32),
    )
    operands = (inv_scale.reshape(1, EMB), slab_embed, slab_probe, point_embed, point_probe)
    return pl.pallas_call(
        kernel,
        name="pathwise_grad",
        out_shape=shapes,
        in_specs=[hbm] * 5,
        out_specs=(vmem, vmem),
        scratch_shapes=[
            pltpu.VMEM((1, EMB), F32),
            pltpu.VMEM(slab_embed.shape, F32),
            pltpu.VMEM(slab_probe.shape, F32),
            pltpu.VMEM(point_embed.shape, F32),
            pltpu.VMEM(point_probe.shape, F32),
            pltpu.VMEM((ROWS, 6 * EMB + 16), BF16),
            pltpu.VMEM((ROWS, 6 * PROBES), BF16),
            pltpu.VMEM((3 * EMB + 16, ROWS), BF16),
            pltpu.VMEM((2, 4, 2, 2, HALF, 128), F32),
            pltpu.VMEM((2, 4, 2, HALF, 128), F32),
            pltpu.VMEM((2, 2, HALF, 128), F32),
            pltpu.VMEM((2, 2, 2, HALF, 128), F32),
            pltpu.VMEM((2, 4, 2, 2, HALF, 128), F32),
            pltpu.VMEM((4, 4, 16, 128), F32),
            pltpu.VMEM((3, 4, 16, 128), F32),
            pltpu.VMEM((4, 16, 128), F32),
            pltpu.VMEM((3, 16, 128), F32),
            pltpu.VMEM((4, 16, 128), F32),
            pltpu.VMEM((4, 4, 16, 128), F32),
            pltpu.SemaphoreType.DMA((5,)),
            pltpu.SemaphoreType.DMA((80,)),
            pltpu.SemaphoreType.DMA((80,)),
        ],
        compiler_params=pltpu.CompilerParams(
            collective_id=0, has_side_effects=True, vmem_limit_bytes=VMEM_MIB * 1024 * 1024
        ),
    )(*(pltpu.with_memory_space_constraint(v, pltpu.HBM) for v in operands))


def solution(mesh):
    placed = (P(None, "row"), P(None, "row"), P(None, "col"), P(None, "col"), P())
    return jax.shard_map(
        local,
        mesh=mesh,
        in_specs=placed,
        out_specs=(P(None, "row"), P(None, "col")),
        check_vma=False,
    )
```

```python
import math

import jax
import jax.numpy as jnp
from jax import lax
from jax.experimental import pallas as pl
from jax.experimental.pallas import tpu as pltpu
from jax.sharding import PartitionSpec as P

MESH = pl.DeviceIdType.MESH
F32 = jnp.float32
BF16 = jnp.bfloat16
LOG2E = math.log2(math.e)
EMB = 64
PROBES = 32
ROWS = 512
PIECE = 512
UNIT = 256
VMEM_MIB = 40
HALF = 32


def split3(v):
    high = v.astype(BF16)
    rest = v - high.astype(F32)
    mid = rest.astype(BF16)
    low = (rest - mid.astype(F32)).astype(BF16)
    return high, mid, low


def matmul(a, b, contract):
    return lax.dot_general(a, b, ((contract[:1], contract[1:]), ((), ())), preferred_element_type=F32)


def kernel(
    scale_hbm,
    slab_hbm,
    slab_probe_hbm,
    point_hbm,
    point_probe_hbm,
    slab_out,
    point_out,
    scale_ref,
    slab_ref,
    slab_probe_ref,
    point_ref,
    point_probe_ref,
    left_c,
    left_p,
    left_s,
    part,
    sib_in,
    r1,
    r2,
    full,
    sp,
    sx_in,
    sx,
    sy_in,
    sz,
    sf,
    load,
    send,
    recv,
):
    row, col = lax.axis_index("row"), lax.axis_index("col")
    core, q = lax.rem(row, 2), row // 2
    zl, x, y = lax.rem(col, 4), lax.rem(col // 4, 4), col // 16
    other = 1 - core
    p_up, p_down, p_far = lax.rem(q + 1, 4), lax.rem(q + 3, 4), lax.rem(q + 2, 4)
    pieces = (p_far, p_up, p_down, q)

    def columns(j, u):
        return pl.ds(pl.multiple_of(pieces[j] * PIECE + u * UNIT, UNIT), UNIT)

    loads = [
        pltpu.make_async_copy(scale_hbm, scale_ref, load.at[0]),
        pltpu.make_async_copy(slab_hbm, slab_ref, load.at[1]),
        pltpu.make_async_copy(slab_probe_hbm, slab_probe_ref, load.at[2]),
        pltpu.make_async_copy(point_hbm, point_ref, load.at[3]),
        pltpu.make_async_copy(point_probe_hbm, point_probe_ref, load.at[4]),
    ]
    for c in loads:
        c.start()

    def at_z(k):
        return (col, lax.rem(q + k, 4) * 2 + core)

    sibling = (col, q * 2 + other)
    z_up, z_down = at_z(1), at_z(3)

    def in_plane(i, k):
        return (lax.rem(y + k, 4) * 16 + lax.rem(x + i, 4) * 4 + zl, row)

    def at_l(k):
        return (y * 16 + x * 4 + lax.rem(zl + k, 4), row)

    partners = [sibling, z_up, z_down]
    for k in (1, 2, 3):
        partners += [in_plane(k, 0), in_plane(0, k), at_l(k)]
    barrier = pltpu.get_barrier_semaphore()
    for device in partners:
        pl.semaphore_signal(barrier, inc=1, device_id=device, device_id_type=MESH)

    sent = []

    def go(src, dst, device):
        i = len(sent)
        c = pltpu.make_async_remote_copy(
            src_ref=src, dst_ref=dst, send_sem=send.at[i], recv_sem=recv.at[i],
            device_id=device, device_id_type=MESH,
        )
        c.start()
        sent.append(c)
        return c

    diag = lax.broadcasted_iota(jnp.int32, (EMB, EMB), 0) == lax.broadcasted_iota(jnp.int32, (EMB, EMB), 1)
    row_id = lax.broadcasted_iota(jnp.int32, (16, ROWS), 0)
    ones = jnp.ones((16, ROWS), BF16)

    def extras(term, first, width):
        ids = row_id[:, :width]
        base = jnp.where(ids < 6, 1.0, 0.0)
        for i, t in enumerate(split3(term)):
            base = jnp.where(ids == first + i, t.astype(F32), base)
        return base.astype(BF16)

    loads[0].wait()
    loads[1].wait()
    scale = jnp.sum(jnp.where(diag, scale_ref[...], 0.0), axis=1, keepdims=True)
    w2 = scale * scale
    slab = slab_ref[...]
    scaled = slab * w2
    self_term = jnp.sum(scaled * slab, axis=0, keepdims=True) * (-0.5 * LOG2E)
    xh, xm, xl = split3(scaled * LOG2E)
    hm = jnp.concatenate([xh, xm], axis=0).T
    left_c[:, 0:128] = hm
    left_c[:, 128:256] = hm
    left_c[:, 256:384] = jnp.concatenate([xh, xl], axis=0).T
    left_c[:, 384:400] = extras(self_term, 0, ROWS).T
    loads[2].wait()
    ph, pm, pl_ = split3(slab_probe_ref[...])
    left_p[:, 0:128] = jnp.concatenate([ph, pm, ph, pm], axis=0).T
    left_p[:, 128:192] = jnp.concatenate([ph, pl_], axis=0).T
    sh, sm, sl = split3(slab)
    left_s[...] = jnp.concatenate([sh, sm, sl, ones], axis=0)
    loads[3].wait()
    loads[4].wait()

    def compute(u, j, total):
        points = point_ref[:, columns(j, u)]
        probes = point_probe_ref[:, columns(j, u)]
        other_term = jnp.sum(w2 * points * points, axis=0, keepdims=True) * (-0.5 * LOG2E)
        yh, ym, yl = split3(points)
        right_c = jnp.concatenate([yh, ym, ym, yh, yl, yh, extras(other_term, 3, UNIT)], axis=0)
        gh, gm, gl = split3(probes)
        right_p = jnp.concatenate([gh, gm, gm, gh, gl, gh], axis=0)
        exponent = matmul(left_c[...], right_c, (1, 0))
        weights = jnp.exp2(exponent) * matmul(left_p[...], right_p, (1, 0))
        mh = weights.astype(BF16)
        ml = (weights - mh.astype(F32)).astype(BF16)
        ls = left_s[...]
        o2 = matmul(jnp.concatenate([ls, ls], axis=1), jnp.concatenate([mh, ml], axis=0), (1, 0))
        right_s = jnp.concatenate([yh, ym, yl, ones[:, :UNIT]], axis=0)
        o1 = matmul(jnp.concatenate([right_s, right_s], axis=1), jnp.concatenate([mh, ml], axis=1), (1, 1))
        mixed = o2[0:64] + o2[64:128] + o2[128:192]
        terms = w2 * (mixed - points * o2[192:193])
        for h in range(2):
            for v in range(2):
                part[u, j, h, v] = terms[h * HALF : h * HALF + HALF, v * 128 : v * 128 + 128]
        return o1 if total is None else total + o1

    def to_sibling(u, j):
        return go(part.at[u, j, other], sib_in.at[u, j], sibling)

    def take(c, u, j):
        c.wait_recv()
        part[u, j, core] = part[u, j, core] + sib_in[u, j]

    def far(u):
        a0 = go(part.at[u, 0, core, 0], r1.at[u, 0], z_down)
        a1 = go(part.at[u, 0, core, 1], r1.at[u, 1], z_up)
        return a0, a1

    def near(u):
        b1 = go(part.at[u, 1, core, 0], r2.at[u, 1, 0], z_up)
        b0 = go(part.at[u, 2, core, 1], r2.at[u, 0, 1], z_down)
        return b0, b1

    def near_sum(u, a):
        a[0].wait_recv()
        part[u, 2, core, 0] = part[u, 2, core, 0] + r1[u, 0]
        b2 = go(part.at[u, 2, core, 0], r2.at[u, 0, 0], z_down)
        a[1].wait_recv()
        part[u, 1, core, 1] = part[u, 1, core, 1] + r1[u, 1]
        b3 = go(part.at[u, 1, core, 1], r2.at[u, 1, 1], z_up)
        return b2, b3

    def share(u, piece, device, v=None):
        block = full.at[u, piece, core] if v is None else full.at[u, piece, core, v]
        return go(block, block, device)

    def finish(u, b, c):
        b[1].wait_recv()
        c[0].wait_recv()
        full[u, q, core, 0] = part[u, 3, core, 0] + r2[u, 0, 0] + r2[u, 1, 0]
        d0 = share(u, q, z_down, 0)
        b[0].wait_recv()
        c[1].wait_recv()
        full[u, q, core, 1] = part[u, 3, core, 1] + r2[u, 0, 1] + r2[u, 1, 1]
        d1 = share(u, q, z_up, 1)
        return d0, d1

    def finish_rest(u, d):
        d2 = share(u, q, z_up, 0)
        d3 = share(u, q, z_down, 1)
        return d + (d2, d3), [share(u, q, sibling)]

    def forward(u, d):
        d[0].wait_recv()
        f0 = share(u, p_up, z_down, 0)
        d[1].wait_recv()
        f1 = share(u, p_down, z_up, 1)
        return f0, f1

    def spread(u, d, e):
        d[2].wait_recv()
        e.append(share(u, p_down, sibling))
        d[3].wait_recv()
        e.append(share(u, p_up, sibling))

    def spread_far(u, f, e):
        f[0].wait_recv()
        e.append(share(u, p_far, sibling, 0))
        f[1].wait_recv()
        e.append(share(u, p_far, sibling, 1))

    def store(u, piece):
        for h in range(2):
            for v in range(2):
                lo = pl.multiple_of(piece * PIECE + u * UNIT + v * 128, 128)
                point_out[h * HALF : h * HALF + HALF, pl.ds(lo, 128)] = full[u, piece, h, v]

    total = compute(0, 0, None)
    pl.semaphore_wait(barrier, len(partners))
    s00 = to_sibling(0, 0)
    total = compute(1, 0, total)
    s10 = to_sibling(1, 0)
    total = compute(0, 1, total)
    s01 = to_sibling(0, 1)
    take(s00, 0, 0)
    a_0 = far(0)
    total = compute(0, 2, total)
    s02 = to_sibling(0, 2)
    take(s10, 1, 0)
    a_1 = far(1)
    total = compute(1, 1, total)
    s11 = to_sibling(1, 1)
    take(s01, 0, 1)
    total = compute(1, 2, total)
    s12 = to_sibling(1, 2)
    take(s02, 0, 2)
    b_0 = near(0)
    total = compute(0, 3, total)
    s03 = to_sibling(0, 3)
    take(s11, 1, 1)
    total = compute(1, 3, total)
    s13 = to_sibling(1, 3)
    take(s12, 1, 2)
    b_1 = near(1)

    slab_mixed = total[0:64] + total[64:128] + total[128:192]
    slab_terms = w2 * (slab_mixed - slab * total[192:193])
    for i in range(4):
        for k in range(4):
            sp[i, k] = slab_terms[16 * i : 16 * i + 16, 128 * k : 128 * k + 128]
    across = [go(sp.at[lax.rem(x + k, 4)], sx_in.at[k - 1], in_plane(k, 0)) for k in (1, 2, 3)]
    c_0 = near_sum(0, a_0)
    c_1 = near_sum(1, a_1)
    take(s03, 0, 3)
    take(s13, 1, 3)
    for c in across:
        c.wait_recv()
    sx[...] = sp[x] + sx_in[0] + sx_in[1] + sx_in[2]
    across = [go(sx.at[lax.rem(y + k, 4)], sy_in.at[k - 1], in_plane(0, k)) for k in (1, 2, 3)]


    d_0 = finish(0, b_0, c_0)
    d_1 = finish(1, b_1, c_1)
    d_0, e_0 = finish_rest(0, d_0)
    d_1, e_1 = finish_rest(1, d_1)
    for c in across:
        c.wait_recv()
    sz[zl] = sx[y] + sy_in[0] + sy_in[1] + sy_in[2]
    along = [go(sz.at[zl], sz.at[zl], at_l(k)) for k in (1, 2, 3)]

    for c in along:
        c.wait_recv()
    sf[x, y] = sz[0] + sz[1] + sz[2] + sz[3]
    gather = [go(sf.at[x, y], sf.at[x, y], in_plane(i, k)) for i in range(4) for k in range(4) if i or k]
    f_0 = forward(0, d_0)
    f_1 = forward(1, d_1)
    spread(0, d_0, e_0)
    spread(1, d_1, e_1)
    for u, e in enumerate((e_0, e_1)):
        for c in e:
            c.wait_recv()
        for j in (1, 2, 3):
            store(u, pieces[j])
    spread_far(0, f_0, e_0)
    spread_far(1, f_1, e_1)
    for c in gather:
        c.wait_recv()
    for i in range(4):
        for k in range(4):
            slab_out[16 * i : 16 * i + 16, 128 * k : 128 * k + 128] = sf[i, k]
    for u, e in enumerate((e_0, e_1)):
        for c in e[3:]:
            c.wait_recv()
        store(u, p_far)
    for c in sent:
        c.wait_send()


def write_kernel(slab, point, slab_out, point_out, sems):
    first = pltpu.make_async_copy(point, point_out, sems.at[0])
    second = pltpu.make_async_copy(slab, slab_out, sems.at[1])
    first.start()
    second.start()
    first.wait()
    second.wait()


def local(slab_embed, slab_probe, point_embed, point_probe, inv_scale):
    vmem = pl.BlockSpec(memory_space=pltpu.VMEM)
    hbm = pl.BlockSpec(memory_space=pltpu.HBM)
    shapes = (
        jax.ShapeDtypeStruct(slab_embed.shape, F32),
        jax.ShapeDtypeStruct(point_embed.shape, F32),
    )
    operands = (inv_scale.reshape(1, EMB), slab_embed, slab_probe, point_embed, point_probe)
    grads = pl.pallas_call(
        kernel,
        name="pathwise_grad",
        out_shape=shapes,
        in_specs=[hbm] * 5,
        out_specs=(vmem, vmem),
        scratch_shapes=[
            pltpu.VMEM((1, EMB), F32),
            pltpu.VMEM(slab_embed.shape, F32),
            pltpu.VMEM(slab_probe.shape, F32),
            pltpu.VMEM(point_embed.shape, F32),
            pltpu.VMEM(point_probe.shape, F32),
            pltpu.VMEM((ROWS, 6 * EMB + 16), BF16),
            pltpu.VMEM((ROWS, 6 * PROBES), BF16),
            pltpu.VMEM((3 * EMB + 16, ROWS), BF16),
            pltpu.VMEM((2, 4, 2, 2, HALF, 128), F32),
            pltpu.VMEM((2, 4, 2, HALF, 128), F32),
            pltpu.VMEM((2, 2, HALF, 128), F32),
            pltpu.VMEM((2, 2, 2, HALF, 128), F32),
            pltpu.VMEM((2, 4, 2, 2, HALF, 128), F32),
            pltpu.VMEM((4, 4, 16, 128), F32),
            pltpu.VMEM((3, 4, 16, 128), F32),
            pltpu.VMEM((4, 16, 128), F32),
            pltpu.VMEM((3, 16, 128), F32),
            pltpu.VMEM((4, 16, 128), F32),
            pltpu.VMEM((4, 4, 16, 128), F32),
            pltpu.SemaphoreType.DMA((5,)),
            pltpu.SemaphoreType.DMA((80,)),
            pltpu.SemaphoreType.DMA((80,)),
        ],
        compiler_params=pltpu.CompilerParams(
            collective_id=0, has_side_effects=True, vmem_limit_bytes=VMEM_MIB * 1024 * 1024
        ),
    )(*(pltpu.with_memory_space_constraint(v, pltpu.HBM) for v in operands))
    return pl.pallas_call(
        write_kernel,
        name="write_out",
        out_shape=shapes,
        in_specs=[vmem] * 2,
        out_specs=(hbm, hbm),
        scratch_shapes=[pltpu.SemaphoreType.DMA((2,))],
    )(*(pltpu.with_memory_space_constraint(v, pltpu.VMEM) for v in grads))


def solution(mesh):
    placed = (P(None, "row"), P(None, "row"), P(None, "col"), P(None, "col"), P())
    return jax.shard_map(
        local,
        mesh=mesh,
        in_specs=placed,
        out_specs=(P(None, "row"), P(None, "col")),
        check_vma=False,
    )
```

```python
import math

import jax
import jax.numpy as jnp
from jax import lax
from jax.experimental import pallas as pl
from jax.experimental.pallas import tpu as pltpu
from jax.sharding import PartitionSpec as P

MESH = pl.DeviceIdType.MESH
F32 = jnp.float32
BF16 = jnp.bfloat16
LOG2E = math.log2(math.e)
EMB = 64
PROBES = 32
ROWS = 512
PIECE = 512
UNIT = 256
VMEM_MIB = 40
HALF = 32


def split3(v):
    high = v.astype(BF16)
    rest = v - high.astype(F32)
    mid = rest.astype(BF16)
    low = (rest - mid.astype(F32)).astype(BF16)
    return high, mid, low


def matmul(a, b, contract):
    return lax.dot_general(a, b, ((contract[:1], contract[1:]), ((), ())), preferred_element_type=F32)


def kernel(
    scale_hbm,
    slab_hbm,
    slab_probe_hbm,
    point_hbm,
    point_probe_hbm,
    slab_out,
    point_out,
    scale_ref,
    slab_ref,
    slab_probe_ref,
    point_ref,
    point_probe_ref,
    left_c,
    left_p,
    left_s,
    part,
    sib_in,
    r1,
    r2,
    full,
    sp,
    sx_in,
    sx,
    sy_in,
    sz,
    sf,
    load,
    send,
    recv,
):
    row, col = lax.axis_index("row"), lax.axis_index("col")
    core, q = lax.rem(row, 2), row // 2
    zl, x, y = lax.rem(col, 4), lax.rem(col // 4, 4), col // 16
    other = 1 - core
    p_up, p_down, p_far = lax.rem(q + 1, 4), lax.rem(q + 3, 4), lax.rem(q + 2, 4)
    pieces = (p_far, p_up, p_down, q)

    def columns(j, u):
        return pl.ds(pl.multiple_of(pieces[j] * PIECE + u * UNIT, UNIT), UNIT)

    loads = [
        pltpu.make_async_copy(scale_hbm, scale_ref, load.at[0]),
        pltpu.make_async_copy(slab_hbm, slab_ref, load.at[1]),
        pltpu.make_async_copy(slab_probe_hbm, slab_probe_ref, load.at[2]),
        pltpu.make_async_copy(point_hbm, point_ref, load.at[3]),
        pltpu.make_async_copy(point_probe_hbm, point_probe_ref, load.at[4]),
    ]
    for c in loads:
        c.start()

    def at_z(k):
        return (col, lax.rem(q + k, 4) * 2 + core)

    sibling = (col, q * 2 + other)
    z_up, z_down = at_z(1), at_z(3)

    def in_plane(i, k):
        return (lax.rem(y + k, 4) * 16 + lax.rem(x + i, 4) * 4 + zl, row)

    def at_l(k):
        return (y * 16 + x * 4 + lax.rem(zl + k, 4), row)

    partners = [sibling, z_up, z_down]
    for k in (1, 2, 3):
        partners += [in_plane(k, 0), in_plane(0, k), at_l(k)]
    barrier = pltpu.get_barrier_semaphore()
    for device in partners:
        pl.semaphore_signal(barrier, inc=1, device_id=device, device_id_type=MESH)

    sent = []

    def go(src, dst, device):
        i = len(sent)
        c = pltpu.make_async_remote_copy(
            src_ref=src, dst_ref=dst, send_sem=send.at[i], recv_sem=recv.at[i],
            device_id=device, device_id_type=MESH,
        )
        c.start()
        sent.append(c)
        return c

    diag = lax.broadcasted_iota(jnp.int32, (EMB, EMB), 0) == lax.broadcasted_iota(jnp.int32, (EMB, EMB), 1)
    row_id = lax.broadcasted_iota(jnp.int32, (16, ROWS), 0)
    ones = jnp.ones((16, ROWS), BF16)

    def extras(term, first, width):
        ids = row_id[:, :width]
        base = jnp.where(ids < 6, 1.0, 0.0)
        for i, t in enumerate(split3(term)):
            base = jnp.where(ids == first + i, t.astype(F32), base)
        return base.astype(BF16)

    loads[0].wait()
    loads[1].wait()
    scale = jnp.sum(jnp.where(diag, scale_ref[...], 0.0), axis=1, keepdims=True)
    w2 = scale * scale
    slab = slab_ref[...]
    scaled = slab * w2
    self_term = jnp.sum(scaled * slab, axis=0, keepdims=True) * (-0.5 * LOG2E)
    xh, xm, xl = split3(scaled * LOG2E)
    hm = jnp.concatenate([xh, xm], axis=0).T
    left_c[:, 0:128] = hm
    left_c[:, 128:256] = hm
    left_c[:, 256:384] = jnp.concatenate([xh, xl], axis=0).T
    left_c[:, 384:400] = extras(self_term, 0, ROWS).T
    loads[2].wait()
    ph, pm, pl_ = split3(slab_probe_ref[...])
    left_p[:, 0:128] = jnp.concatenate([ph, pm, ph, pm], axis=0).T
    left_p[:, 128:192] = jnp.concatenate([ph, pl_], axis=0).T
    sh, sm, sl = split3(slab)
    left_s[...] = jnp.concatenate([sh, sm, sl, ones], axis=0)
    loads[3].wait()
    loads[4].wait()

    def compute(u, j, total):
        points = point_ref[:, columns(j, u)]
        probes = point_probe_ref[:, columns(j, u)]
        other_term = jnp.sum(w2 * points * points, axis=0, keepdims=True) * (-0.5 * LOG2E)
        yh, ym, yl = split3(points)
        right_c = jnp.concatenate([yh, ym, ym, yh, yl, yh, extras(other_term, 3, UNIT)], axis=0)
        gh, gm, gl = split3(probes)
        right_p = jnp.concatenate([gh, gm, gm, gh, gl, gh], axis=0)
        exponent = matmul(left_c[...], right_c, (1, 0))
        weights = jnp.exp2(exponent) * matmul(left_p[...], right_p, (1, 0))
        mh = weights.astype(BF16)
        ml = (weights - mh.astype(F32)).astype(BF16)
        ls = left_s[...]
        o2 = matmul(jnp.concatenate([ls, ls], axis=1), jnp.concatenate([mh, ml], axis=0), (1, 0))
        right_s = jnp.concatenate([yh, ym, yl, ones[:, :UNIT]], axis=0)
        o1 = matmul(jnp.concatenate([right_s, right_s], axis=1), jnp.concatenate([mh, ml], axis=1), (1, 1))
        mixed = o2[0:64] + o2[64:128] + o2[128:192]
        terms = w2 * (mixed - points * o2[192:193])
        for h in range(2):
            for v in range(2):
                part[u, j, h, v] = terms[h * HALF : h * HALF + HALF, v * 128 : v * 128 + 128]
        return o1 if total is None else total + o1

    def to_sibling(u, j):
        return go(part.at[u, j, other], sib_in.at[u, j], sibling)

    def take(c, u, j):
        c.wait_recv()
        part[u, j, core] = part[u, j, core] + sib_in[u, j]

    def far(u):
        a0 = go(part.at[u, 0, core, 0], r1.at[u, 0], z_down)
        a1 = go(part.at[u, 0, core, 1], r1.at[u, 1], z_up)
        return a0, a1

    def near(u):
        b1 = go(part.at[u, 1, core, 0], r2.at[u, 1, 0], z_up)
        b0 = go(part.at[u, 2, core, 1], r2.at[u, 0, 1], z_down)
        return b0, b1

    def near_sum(u, a):
        a[0].wait_recv()
        part[u, 2, core, 0] = part[u, 2, core, 0] + r1[u, 0]
        b2 = go(part.at[u, 2, core, 0], r2.at[u, 0, 0], z_down)
        a[1].wait_recv()
        part[u, 1, core, 1] = part[u, 1, core, 1] + r1[u, 1]
        b3 = go(part.at[u, 1, core, 1], r2.at[u, 1, 1], z_up)
        return b2, b3

    def share(u, piece, device, v=None):
        block = full.at[u, piece, core] if v is None else full.at[u, piece, core, v]
        return go(block, block, device)

    def finish(u, b, c):
        b[1].wait_recv()
        c[0].wait_recv()
        full[u, q, core, 0] = part[u, 3, core, 0] + r2[u, 0, 0] + r2[u, 1, 0]
        d0 = share(u, q, z_down, 0)
        b[0].wait_recv()
        c[1].wait_recv()
        full[u, q, core, 1] = part[u, 3, core, 1] + r2[u, 0, 1] + r2[u, 1, 1]
        d1 = share(u, q, z_up, 1)
        return d0, d1

    def finish_rest(u, d):
        d2 = share(u, q, z_up, 0)
        d3 = share(u, q, z_down, 1)
        return d + (d2, d3), [share(u, q, sibling)]

    def forward(u, d):
        d[0].wait_recv()
        f0 = share(u, p_up, z_down, 0)
        d[1].wait_recv()
        f1 = share(u, p_down, z_up, 1)
        return f0, f1

    def spread(u, d, e):
        d[2].wait_recv()
        e.append(share(u, p_down, sibling))
        d[3].wait_recv()
        e.append(share(u, p_up, sibling))

    def spread_far(u, f, e):
        f[0].wait_recv()
        e.append(share(u, p_far, sibling, 0))
        f[1].wait_recv()
        e.append(share(u, p_far, sibling, 1))

    def store(u, piece):
        for h in range(2):
            for v in range(2):
                lo = pl.multiple_of(piece * PIECE + u * UNIT + v * 128, 128)
                point_out[h * HALF : h * HALF + HALF, pl.ds(lo, 128)] = full[u, piece, h, v]

    total = compute(0, 0, None)
    pl.semaphore_wait(barrier, len(partners))
    s00 = to_sibling(0, 0)
    total = compute(1, 0, total)
    s10 = to_sibling(1, 0)
    total = compute(0, 1, total)
    s01 = to_sibling(0, 1)
    take(s00, 0, 0)
    a_0 = far(0)
    total = compute(0, 2, total)
    s02 = to_sibling(0, 2)
    take(s10, 1, 0)
    a_1 = far(1)
    total = compute(1, 1, total)
    s11 = to_sibling(1, 1)
    take(s01, 0, 1)
    total = compute(1, 2, total)
    s12 = to_sibling(1, 2)
    take(s02, 0, 2)
    b_0 = near(0)
    total = compute(0, 3, total)
    s03 = to_sibling(0, 3)
    take(s11, 1, 1)
    total = compute(1, 3, total)
    s13 = to_sibling(1, 3)
    take(s12, 1, 2)
    b_1 = near(1)

    slab_mixed = total[0:64] + total[64:128] + total[128:192]
    slab_terms = w2 * (slab_mixed - slab * total[192:193])
    for i in range(4):
        for k in range(4):
            sp[i, k] = slab_terms[16 * i : 16 * i + 16, 128 * k : 128 * k + 128]
    across = [go(sp.at[lax.rem(x + k, 4)], sx_in.at[k - 1], in_plane(k, 0)) for k in (1, 2, 3)]
    c_0 = near_sum(0, a_0)
    c_1 = near_sum(1, a_1)
    take(s03, 0, 3)
    take(s13, 1, 3)
    for c in across:
        c.wait_recv()
    sx[...] = sp[x] + sx_in[0] + sx_in[1] + sx_in[2]
    across = [go(sx.at[lax.rem(y + k, 4)], sy_in.at[k - 1], in_plane(0, k)) for k in (1, 2, 3)]


    d_0 = finish(0, b_0, c_0)
    d_1 = finish(1, b_1, c_1)
    d_0, e_0 = finish_rest(0, d_0)
    d_1, e_1 = finish_rest(1, d_1)
    for c in across:
        c.wait_recv()
    sz[zl] = sx[y] + sy_in[0] + sy_in[1] + sy_in[2]
    along = [go(sz.at[zl], sz.at[zl], at_l(k)) for k in (1, 2, 3)]

    for c in along:
        c.wait_recv()
    sf[x, y] = sz[0] + sz[1] + sz[2] + sz[3]
    gather = [go(sf.at[x, y], sf.at[x, y], in_plane(i, k)) for i in range(4) for k in range(4) if i or k]
    f_0 = forward(0, d_0)
    f_1 = forward(1, d_1)
    spread(0, d_0, e_0)
    spread(1, d_1, e_1)
    for u, e in enumerate((e_0, e_1)):
        for c in e:
            c.wait_recv()
        for j in (1, 2, 3):
            store(u, pieces[j])
    spread_far(0, f_0, e_0)
    spread_far(1, f_1, e_1)
    for u, e in enumerate((e_0, e_1)):
        for c in e[3:]:
            c.wait_recv()
        store(u, p_far)
    for c in gather:
        c.wait_recv()
    for i in range(4):
        for k in range(4):
            slab_out[16 * i : 16 * i + 16, 128 * k : 128 * k + 128] = sf[i, k]
    for c in sent:
        c.wait_send()


def write_kernel(slab, point, slab_out, point_out, sems):
    first = pltpu.make_async_copy(point, point_out, sems.at[0])
    second = pltpu.make_async_copy(slab, slab_out, sems.at[1])
    first.start()
    second.start()
    first.wait()
    second.wait()


def local(slab_embed, slab_probe, point_embed, point_probe, inv_scale):
    vmem = pl.BlockSpec(memory_space=pltpu.VMEM)
    hbm = pl.BlockSpec(memory_space=pltpu.HBM)
    shapes = (
        jax.ShapeDtypeStruct(slab_embed.shape, F32),
        jax.ShapeDtypeStruct(point_embed.shape, F32),
    )
    operands = (inv_scale.reshape(1, EMB), slab_embed, slab_probe, point_embed, point_probe)
    grads = pl.pallas_call(
        kernel,
        name="pathwise_grad",
        out_shape=shapes,
        in_specs=[hbm] * 5,
        out_specs=(vmem, vmem),
        scratch_shapes=[
            pltpu.VMEM((1, EMB), F32),
            pltpu.VMEM(slab_embed.shape, F32),
            pltpu.VMEM(slab_probe.shape, F32),
            pltpu.VMEM(point_embed.shape, F32),
            pltpu.VMEM(point_probe.shape, F32),
            pltpu.VMEM((ROWS, 6 * EMB + 16), BF16),
            pltpu.VMEM((ROWS, 6 * PROBES), BF16),
            pltpu.VMEM((3 * EMB + 16, ROWS), BF16),
            pltpu.VMEM((2, 4, 2, 2, HALF, 128), F32),
            pltpu.VMEM((2, 4, 2, HALF, 128), F32),
            pltpu.VMEM((2, 2, HALF, 128), F32),
            pltpu.VMEM((2, 2, 2, HALF, 128), F32),
            pltpu.VMEM((2, 4, 2, 2, HALF, 128), F32),
            pltpu.VMEM((4, 4, 16, 128), F32),
            pltpu.VMEM((3, 4, 16, 128), F32),
            pltpu.VMEM((4, 16, 128), F32),
            pltpu.VMEM((3, 16, 128), F32),
            pltpu.VMEM((4, 16, 128), F32),
            pltpu.VMEM((4, 4, 16, 128), F32),
            pltpu.SemaphoreType.DMA((5,)),
            pltpu.SemaphoreType.DMA((80,)),
            pltpu.SemaphoreType.DMA((80,)),
        ],
        compiler_params=pltpu.CompilerParams(
            collective_id=0, has_side_effects=True, vmem_limit_bytes=VMEM_MIB * 1024 * 1024
        ),
    )(*(pltpu.with_memory_space_constraint(v, pltpu.HBM) for v in operands))
    return pl.pallas_call(
        write_kernel,
        name="write_out",
        out_shape=shapes,
        in_specs=[vmem] * 2,
        out_specs=(hbm, hbm),
        scratch_shapes=[pltpu.SemaphoreType.DMA((2,))],
    )(*(pltpu.with_memory_space_constraint(v, pltpu.VMEM) for v in grads))


def solution(mesh):
    placed = (P(None, "row"), P(None, "row"), P(None, "col"), P(None, "col"), P())
    return jax.shard_map(
        local,
        mesh=mesh,
        in_specs=placed,
        out_specs=(P(None, "row"), P(None, "col")),
        check_vma=False,
    )
```
